128 devices in a mesh: alpha: 64 (over z, y, x), beta: 2 (over core).
Axes of the slice: x: 4, y: 4, z: 4, core: 2. Of those that a mesh axis runs over, the one named last changes fastest.
Arguments:
- coeffs: bfloat16 [4096, 512], P('alpha', 'beta'), may hold values from -6 to 6
- integrals: bfloat16 [484, 484], replicated, may hold values from -0.0234375 to 0.0234375
- send_block: int32 [64, 512], P('alpha'), may hold values from 0 to 16, as said below
- alpha_slot: int32 [1024, 132], P('alpha'), may hold values from 0 to 255, as said below
- alpha_pair: int32 [1024, 132], P('alpha'), may hold values from 0 to 483, as said below
- alpha_parity: int32 [1024, 132], P('alpha'), may hold values from 0 to 1
- beta_pair: int32 [32, 132], P('beta'), may hold values from 0 to 483, as said below
- beta_target: int32 [32, 132], P('beta'), may hold values from 0 to 31
- beta_parity: int32 [32, 132], P('beta'), may hold values from 0 to 1
Outputs:
- sigma: float32 [4096, 512], P('alpha', 'beta')
The draws below stay inside these ranges and needn't reach their ends.
Inputs may be any that keep to these rules, and one draw needn't show every extreme that they name: `send_block`: in each batch the filled slots from one sender to one receiver come first; at most 4 are filled, 4 is reached from every sender to some receiver in every batch, and some slots stay empty in every batch. `alpha_slot`: every entry names a slot that holds a block. `alpha_pair`: the pairs of one row are distinct. `beta_pair`: the pairs of one row are distinct.
All inputs are finite; a program needn't handle non-finite values.
Results may differ from the reference program's by a relative error of at most 0.0003.
Values may be sent and summed in bfloat16 or wider, within the bound.
A program may use at most 64 MiB of HBM per device.

```python
import jax
import jax.numpy as jnp
from jax import lax

P_SIZE = 484
EXC_BLK = 132
EXCB = 132
SB = 4
BBLK = 16
BATCHES = 2
CAP = 4
BLK_DEV = 16
BLK_BATCH = 8
SLOTS = 256
ABLOCKS = 1024
NA = 4096
NB = 512
NBLKB = 32
N_ALPHA = 64


def alpha_plan(key):
    base = jax.random.fold_in(key, 7)
    key_count, key_busy, key_block, key_sender, key_cell, key_quiet = jax.random.split(base, 6)
    counts = jax.random.randint(key_count, (BATCHES, N_ALPHA, N_ALPHA), 1, CAP + 1)
    busy = jax.random.randint(key_busy, (BATCHES,), 0, N_ALPHA)
    quiet = jax.random.randint(key_quiet, (BATCHES, N_ALPHA), 0, N_ALPHA)
    receivers = jnp.arange(N_ALPHA, dtype=jnp.int32)
    senders_all = jnp.arange(N_ALPHA, dtype=jnp.int32)
    silent = (senders_all[None, :, None] == quiet[:, None, :]) & (receivers[None, None, :] != busy[:, None, None])
    counts = jnp.where(silent, 0, counts)
    counts = jnp.where(receivers[None, None, :] == busy[:, None, None], CAP, counts)
    chosen = jax.random.randint(key_block, (BATCHES, N_ALPHA, N_ALPHA, CAP), 0, BLK_DEV)
    cells = jnp.arange(CAP, dtype=jnp.int32)
    filled = cells[None, None, None, :] < counts[..., None]
    sending = jnp.where(filled, chosen, BLK_DEV)
    send_table = sending.transpose(1, 0, 2, 3).reshape(N_ALPHA, BATCHES * N_ALPHA * CAP)
    batch_of = jnp.arange(BLK_DEV, dtype=jnp.int32) // (BLK_DEV // BATCHES)
    owners = jnp.arange(N_ALPHA, dtype=jnp.int32)
    quiet_here = quiet[batch_of[None, :, None], owners[:, None, None]]
    raw_sender = jax.random.randint(key_sender, (N_ALPHA, BLK_DEV, EXC_BLK), 0, N_ALPHA - 1)
    sender = raw_sender + (raw_sender >= quiet_here).astype(jnp.int32)
    raw_cell = jax.random.randint(key_cell, (N_ALPHA, BLK_DEV, EXC_BLK), 0, 1 << 20)
    count_here = counts[batch_of[None, :, None], sender, owners[:, None, None]]
    cell_pick = raw_cell % jnp.maximum(count_here, 1)
    slot_table = (sender * CAP + cell_pick).reshape(N_ALPHA * BLK_DEV, EXC_BLK)
    return (send_table.astype(jnp.int32), slot_table.astype(jnp.int32))


def distinct_pairs(key, row_count, pick_count):
    scores = jax.random.randint(key, (row_count, P_SIZE), 0, 1 << 20) * P_SIZE + jnp.arange(P_SIZE, dtype=jnp.int32)[None, :]
    return jnp.argsort(scores, axis=1)[:, :pick_count].astype(jnp.int32)


def draw_send_block(key, part):
    return alpha_plan(key)[0]


def draw_alpha_slot(key, part):
    return alpha_plan(key)[1]


def draw_alpha_pair(key, part):
    return distinct_pairs(jax.random.fold_in(key, 11), ABLOCKS, EXC_BLK)


def draw_beta_pair(key, part):
    return distinct_pairs(jax.random.fold_in(key, 13), NBLKB, EXCB)


def touch_ends(values, rng, least, top_value):
    longest = values.shape.index(max(values.shape))
    spots = []
    for shift in (0, 1):
        where = [jax.random.randint(jax.random.fold_in(rng, axis), (), 0, length) for axis, length in enumerate(values.shape)]
        where[longest] = (where[longest] + shift) % values.shape[longest]
        spots.append(tuple(where))
    return values.at[spots[0]].set(least).at[spots[1]].set(top_value)


def steps_of(own_key, extent, cuts, smallest, largest):
    def one(axis_at, blocks):
        draws = jax.random.uniform(jax.random.fold_in(jax.random.fold_in(own_key, 6), axis_at), (blocks,), jnp.float32, smallest / len(cuts), largest / len(cuts))
        return jnp.repeat(jnp.exp(draws), extent[axis_at] // blocks).reshape((-1,) + (1,) * (len(extent) - axis_at - 1))

    level = one(*cuts[0])
    for cut in cuts[1:]:
        level = level * one(*cut)
    return level


def noise(rng, shape, spread, limit, cuts=(), kind=jnp.bfloat16):
    array = jax.random.normal(rng, shape, jnp.float32) * spread
    if len(cuts) > 0:
        array = steps_of(rng, shape, cuts, -0.22, 0.18) * array
    return jnp.clip(array, min=-limit, max=limit).astype(kind)


def setup_inputs(seed: int = 0) -> dict:
    keys = jax.random.split(jax.random.key(seed), 10)
    return {
        "coeffs": noise(keys[0], (NA, NB), 1.0, 6.0, ((0, 64), (1, 2))),
        "integrals": noise(keys[1], (P_SIZE, P_SIZE), (P_SIZE * EXCB) ** -0.5, 0.0234375),
        "send_block": draw_send_block(jax.random.fold_in(keys[9], 71), 0),
        "alpha_slot": draw_alpha_slot(jax.random.fold_in(keys[9], 71), 0),
        "alpha_pair": draw_alpha_pair(jax.random.fold_in(keys[9], 71), 0),
        "alpha_parity": touch_ends(jax.random.randint(keys[5], (ABLOCKS, EXC_BLK), 0, 2), jax.random.fold_in(keys[5], 1), 0, 1).astype(jnp.int32),
        "beta_pair": draw_beta_pair(jax.random.fold_in(keys[9], 71), 0),
        "beta_target": touch_ends(jax.random.randint(keys[7], (NBLKB, EXCB), 0, NBLKB), jax.random.fold_in(keys[7], 1), 0, NBLKB - 1).astype(jnp.int32),
        "beta_parity": touch_ends(jax.random.randint(keys[8], (NBLKB, EXCB), 0, 2), jax.random.fold_in(keys[8], 1), 0, 1).astype(jnp.int32),
    }


def reference(coeffs, integrals, send_block, alpha_slot, alpha_pair, alpha_parity, beta_pair, beta_target, beta_parity):
    shaped = coeffs.reshape(N_ALPHA, BLK_DEV, SB, NB)
    empty_row = jnp.zeros((N_ALPHA, 1, SB, NB), coeffs.dtype)
    padded = jnp.concatenate([shaped, empty_row], axis=1)
    beta_factor = (1 - 2 * beta_parity).astype(jnp.float32)
    flat_target = beta_target.reshape(-1)

    def one_block(global_block):
        device = global_block // BLK_DEV
        local_block = global_block % BLK_DEV
        batch_index = local_block // BLK_BATCH
        slots = alpha_slot[global_block]
        sender = slots // CAP
        cell_index = slots % CAP
        column = batch_index * SLOTS + device * CAP + cell_index
        chosen = send_block[sender, column]
        rows_taken = padded[sender, chosen]
        factor = (1 - 2 * alpha_parity[global_block]).astype(coeffs.dtype)
        signed = rows_taken * factor[:, None, None]
        selected = integrals[:, alpha_pair[global_block]]
        contracted = jnp.dot(selected.astype(jnp.float32), signed.reshape(EXC_BLK, SB * NB).astype(jnp.float32), precision=lax.Precision.HIGHEST)
        arranged = contracted.reshape(P_SIZE, SB, NBLKB, BBLK).transpose(2, 0, 1, 3)
        picked = jnp.take_along_axis(arranged, beta_pair[:, :, None, None], axis=1)
        picked = picked * beta_factor[:, :, None, None]
        summed = jax.ops.segment_sum(picked.reshape(NBLKB * EXCB, SB, BBLK), flat_target, num_segments=NBLKB)
        return summed.transpose(1, 0, 2).reshape(SB, NB)

    result = lax.map(one_block, jnp.arange(ABLOCKS, dtype=jnp.int32))
    return result.reshape(NA, NB)
```

```python
import functools

import jax
import jax.numpy as jnp
from jax import lax
from jax.experimental import pallas as pl
from jax.experimental.pallas import tpu as pltpu
from jax.sharding import PartitionSpec as P

MESH = pl.DeviceIdType.MESH
PAIRS = 484
PPAD = 512
EXC = 132
EPAD = 136
SB = 4
BATCHES = 2
CAP = 4
NV = 16
NU = 32
NG = 16
GB = 8
NS = 64
WCH = 8
SLOTS = NS * CAP
F32 = jnp.float32
BF16 = jnp.bfloat16


def kernel(
    coeffs_ref,
    integrals_ref,
    send_ref,
    aslot_ref,
    apair_ref,
    apar_ref,
    bpair_ref,
    btarget_ref,
    bpar_ref,
    out_ref,
    cscr,
    src,
    dst,
    tab,
    codes,
    tscr,
    ipad,
    wscr,
    alhs,
    xscr,
    part,
    rpart,
    ssem,
    rsem,
    lsem,
    psem,
    qsem,
):
    a = lax.axis_index("alpha")
    b = lax.axis_index("beta")
    partner = (a, 1 - b)
    barrier = pltpu.get_barrier_semaphore()

    def signal_peer(k, carry):
        pl.semaphore_signal(barrier, inc=1, device_id=(lax.rem(a + k, NS), b), device_id_type=MESH)
        return carry

    lax.fori_loop(1, NS, signal_peer, 0)
    pl.semaphore_signal(barrier, inc=1, device_id=partner, device_id_type=MESH)

    for h in range(2):
        cscr[h] = coeffs_ref[:, h * 128 : (h + 1) * 128].astype(F32)
    lane_group = lax.broadcasted_iota(jnp.int32, (16, 128), 1) // 16
    pieces = [
        [cscr.at[h][pl.ds(s, 16, stride=SB), :] for h in range(2)] for s in range(SB)
    ]
    columns = []
    for w in range(WCH):
        value = jnp.zeros((16, 128), F32)
        for par in range(2):
            v = 2 * w + par
            for s in range(SB):
                shift = ((par * 4 + s) - (v % 8)) % 8 * 16
                piece = pieces[s][v // 8]
                moved = pltpu.roll(piece, shift, 1) if shift else piece
                value = jnp.where(lane_group == par * 4 + s, moved, value)
        columns.append(value.astype(BF16))
    blocks = jnp.concatenate(columns, axis=1)
    for batch in range(BATCHES):
        wanted = send_ref[:, pl.ds(batch * SLOTS, SLOTS)]
        hot = (lax.broadcasted_iota(jnp.int32, (16, SLOTS), 0) == wanted).astype(F32)
        picked = jnp.dot(hot.T.astype(BF16), blocks, preferred_element_type=F32).astype(BF16)
        for w in range(WCH):
            src[batch, w] = picked[:, w * 128 : (w + 1) * 128].reshape(NS, CAP, 128)

    pl.semaphore_wait(barrier, NS)

    def block_copy(batch, to):
        return pltpu.make_async_remote_copy(
            src_ref=src.at[batch, :, to],
            dst_ref=dst.at[batch, :, a],
            send_sem=ssem.at[batch],
            recv_sem=rsem.at[batch],
            device_id=(to, b),
            device_id_type=MESH,
        )

    for batch in range(BATCHES):

        def send(k, carry):
            block_copy(batch, lax.rem(a + k, NS)).start()
            return carry

        lax.fori_loop(1, NS, send, 0)
    own = [
        pltpu.make_async_copy(src.at[batch, :, a], dst.at[batch, :, a], lsem.at[batch])
        for batch in range(BATCHES)
    ]
    for copy in own:
        copy.start()

    tab[...] = jnp.full(tab.shape, -1.0, F32)
    tab[0, :, 0:EXC] = bpair_ref[...].astype(F32)
    tab[1, :, 0:EXC] = ((1 - 2 * bpar_ref[...]) * (btarget_ref[...] + 1)).astype(F32)
    tab[2, :, 0:EXC] = apair_ref[...].astype(F32)
    tab[3, :, 0:EXC] = ((1 - 2 * apar_ref[...]) * (aslot_ref[...] + 1)).astype(F32)
    pair_lane = lax.broadcasted_iota(jnp.int32, (EPAD, PPAD), 1).astype(F32)
    for side in range(2):
        pair_cols = tab[2 * side].T[0:EPAD]
        code_cols = tab[2 * side + 1].T[0:EPAD]
        for row in range(NV):
            hit = pair_cols[:, row : row + 1] == pair_lane
            codes[side, row] = jnp.sum(
                jnp.where(hit, code_cols[:, row : row + 1], 0.0), axis=0, keepdims=True
            )

    def signed_hot(code, count):
        place = (lax.broadcasted_iota(jnp.int32, (count, PPAD), 0) + 1).astype(F32)
        return (jnp.where(code == place, 1.0, 0.0) - jnp.where(code == -place, 1.0, 0.0)).astype(
            BF16
        )

    def beta_row(v, carry):
        tscr[pl.ds(pl.multiple_of(v * NU, NU), NU), :] = signed_hot(codes[0, v], NU)
        return carry

    lax.fori_loop(0, NV, beta_row, 0)
    ipad[...] = jnp.zeros(ipad.shape, BF16)
    ipad[0:PAIRS, 0:PAIRS] = integrals_ref[...]
    table = jnp.dot(tscr[...], ipad[...], preferred_element_type=F32)
    high = table.astype(BF16)
    wscr[:, 0:PPAD] = high
    wscr[:, PPAD:] = (table - high.astype(F32)).astype(BF16)

    def alpha_row(g, carry):
        hot = signed_hot(codes[1, g], SLOTS)
        product = lax.dot_general(
            wscr[...],
            jnp.concatenate([hot, hot], axis=1),
            (((1,), (1,)), ((), ())),
            preferred_element_type=F32,
        )
        top = product.astype(BF16)
        rest = (product - top.astype(F32)).astype(BF16)
        batch, local = g // GB, lax.rem(g, GB)
        for v in range(NV):
            rows = slice(v * NU, (v + 1) * NU)
            lanes = slice((v // 2) * SLOTS, (v // 2 + 1) * SLOTS)
            alhs[batch, v % 2, local, 0, :, lanes] = top[rows]
            alhs[batch, v % 2, local, 1, :, lanes] = rest[rows]
        return carry

    lax.fori_loop(0, NG, alpha_row, 0)

    small_group = lax.broadcasted_iota(jnp.int32, (GB, 128), 1) // 16
    for batch in range(BATCHES):
        own[batch].wait()
        arrived = pltpu.make_async_remote_copy(
            src_ref=src.at[batch, :, pl.ds(0, NS - 1)],
            dst_ref=dst.at[batch, :, pl.ds(0, NS - 1)],
            send_sem=ssem.at[batch],
            recv_sem=rsem.at[batch],
            device_id=partner,
            device_id_type=MESH,
        )
        arrived.wait_recv()
        right = dst[batch].reshape(WCH * SLOTS, 128)
        left = alhs[batch].reshape(2 * GB * 2 * NU, WCH * SLOTS)
        result = jnp.dot(left, right, preferred_element_type=F32).reshape(2, GB, 2, NU, 128)
        result = result[:, :, 0] + result[:, :, 1]
        even = result[0].reshape(GB * NU, 128)
        odd = result[1].reshape(GB * NU, 128)
        xscr[...] = even + pltpu.roll(odd, 64, 1)
        for j in range(4):
            by_u = [xscr[pl.ds(8 * j + i, GB, stride=NU), :] for i in range(8)]
            total = [jnp.zeros((GB, 128), F32) for _ in range(SB)]
            for d in range(8):
                mixed = by_u[d % 8]
                for s in range(1, SB):
                    mixed = jnp.where(small_group == s, by_u[(s + d) % 8], mixed)
                moved = pltpu.roll(mixed, 16 * d, 1) if d else mixed
                for s in range(SB):
                    total[s] = jnp.where(small_group == (s + d) % 8, moved, total[s])
            for s in range(SB):
                part.at[j // 2, j % 2][pl.ds(batch * GB * SB + s, GB, stride=SB), :] = total[s]

    swap = pltpu.make_async_remote_copy(
        src_ref=part.at[1 - b],
        dst_ref=rpart,
        send_sem=psem,
        recv_sem=qsem,
        device_id=partner,
        device_id_type=MESH,
    )
    swap.start()
    for batch in range(BATCHES):
        pltpu.make_async_remote_copy(
            src_ref=src.at[batch, :, pl.ds(0, NS - 1)],
            dst_ref=dst.at[batch, :, pl.ds(0, NS - 1)],
            send_sem=ssem.at[batch],
            recv_sem=rsem.at[batch],
            device_id=partner,
            device_id_type=MESH,
        ).wait_send()
    swap.wait()
    for h in range(2):
        out_ref[:, h * 128 : (h + 1) * 128] = part[b, h] + rpart[h]


def on_device(*operands):
    vmem = pl.BlockSpec(memory_space=pltpu.VMEM)
    return pl.pallas_call(
        kernel,
        out_shape=jax.ShapeDtypeStruct((64, 256), F32),
        in_specs=[vmem] * 9,
        out_specs=vmem,
        scratch_shapes=[
            pltpu.VMEM((2, 64, 128), F32),
            pltpu.VMEM((BATCHES, WCH, NS, CAP, 128), BF16),
            pltpu.VMEM((BATCHES, WCH, NS, CAP, 128), BF16),
            pltpu.VMEM((4, 16, 256), F32),
            pltpu.VMEM((2, NV, 1, PPAD), F32),
            pltpu.VMEM((NV * NU, PPAD), BF16),
            pltpu.VMEM((PPAD, PPAD), BF16),
            pltpu.VMEM((NV * NU, 2 * PPAD), BF16),
            pltpu.VMEM((BATCHES, 2, GB, 2, NU, WCH * SLOTS), BF16),
            pltpu.VMEM((GB * NU, 128), F32),
            pltpu.VMEM((2, 2, 64, 128), F32),
            pltpu.VMEM((2, 64, 128), F32),
            pltpu.SemaphoreType.DMA((BATCHES,)),
            pltpu.SemaphoreType.DMA((BATCHES,)),
            pltpu.SemaphoreType.DMA((BATCHES,)),
            pltpu.SemaphoreType.DMA,
            pltpu.SemaphoreType.DMA,
        ],
        compiler_params=pltpu.CompilerParams(
            collective_id=0, has_side_effects=True, vmem_limit_bytes=56 << 20
        ),
    )(*operands)


def solution(mesh):
    in_specs = (
        P("alpha", "beta"),
        P(),
        P("alpha", None),
        P("alpha", None),
        P("alpha", None),
        P("alpha", None),
        P("beta", None),
        P("beta", None),
        P("beta", None),
    )
    return jax.shard_map(
        on_device, mesh=mesh, in_specs=in_specs, out_specs=P("alpha", "beta"), check_vma=False
    )
```

```python
import functools

import jax
import jax.numpy as jnp
from jax import lax
from jax.experimental import pallas as pl
from jax.experimental.pallas import tpu as pltpu
from jax.sharding import PartitionSpec as P

MESH = pl.DeviceIdType.MESH
PAIRS = 484
PPAD = 512
EXC = 132
EPAD = 136
SB = 4
BATCHES = 2
CAP = 4
NV = 16
NU = 32
NG = 16
GB = 8
NS = 64
X_LINE, Y_LINE, Z_LINE = (1, 2, 3), (4, 8, 12), (16, 32, 48)
LINES = X_LINE + Y_LINE + Z_LINE


def dims_of(k):
    return (k % 4 > 0) + (k // 4 % 4 > 0) + (k // 16 > 0)


PLANES = tuple(k for k in range(1, 64) if dims_of(k) == 2)
REST = tuple(k for k in range(1, 64) if dims_of(k) == 3)
CHUNKS = ((0, 0, 8), (1, 0, 4), (1, 4, 4))
WCH = 8
SLOTS = NS * CAP
GSTEP = 4
F32 = jnp.float32
BF16 = jnp.bfloat16


def kernel(
    coeffs_ref,
    integrals_ref,
    send_ref,
    aslot_ref,
    apair_ref,
    apar_ref,
    bpair_ref,
    btarget_ref,
    bpar_ref,
    own_ref,
    far_ref,
    coeffs,
    integrals,
    sends,
    small,
    cscr,
    src,
    dst,
    tab,
    codes,
    tscr,
    ipad,
    wscr,
    alhs,
    hots,
    fsum,
    xscr,
    part,
    near_sem,
    wide_sem,
    insem,
    ssem,
    rsem,
    lsem,
    ksem,
    psem,
    qsem,
):
    a = lax.axis_index("alpha")
    b = lax.axis_index("beta")
    partner = (a, 1 - b)

    here = (lax.div(a, 16), lax.rem(lax.div(a, 4), 4), lax.rem(a, 4))
    steps = [[lax.rem(place + i, 4) * scale for i in range(4)] for place, scale in zip(here, (16, 4, 1))]

    def peer(k):
        return steps[0][k // 16] + (steps[1][k // 4 % 4] + steps[2][k % 4])

    barrier = pltpu.get_barrier_semaphore()
    loads = [
        pltpu.make_async_copy(ref, to, insem.at[i])
        for i, (ref, to) in enumerate(
            [(coeffs_ref, coeffs), (send_ref, sends)]
            + [
                (ref, small.at[i])
                for i, ref in enumerate(
                    [bpair_ref, btarget_ref, bpar_ref, apair_ref, aslot_ref, apar_ref]
                )
            ]
            + [(integrals_ref, integrals)]
        )
    ]
    for load in loads:
        load.start()

    def tell(semaphore, k):
        pl.semaphore_signal(semaphore, inc=1, device_id=(peer(k), b), device_id_type=MESH)

    for k in LINES:
        tell(barrier, k)
    pl.semaphore_signal(barrier, inc=1, device_id=partner, device_id_type=MESH)

    loads[0].wait()
    loads[1].wait()
    for h in range(2):
        cscr[h] = coeffs[:, h * 128 : (h + 1) * 128].astype(F32)
    lane_group = lax.broadcasted_iota(jnp.int32, (16, 128), 1) // 16
    pieces = [
        [cscr.at[h][pl.ds(s, 16, stride=SB), :] for h in range(2)] for s in range(SB)
    ]
    columns = []
    for w in range(WCH):
        value = jnp.zeros((16, 128), F32)
        for par in range(2):
            v = 2 * w + par
            for s in range(SB):
                shift = ((par * 4 + s) - (v % 8)) % 8 * 16
                piece = pieces[s][v // 8]
                moved = pltpu.roll(piece, shift, 1) if shift else piece
                value = jnp.where(lane_group == par * 4 + s, moved, value)
        columns.append(value.astype(BF16))
    blocks = jnp.concatenate(columns, axis=1)
    for batch in range(BATCHES):
        wanted = sends[:, pl.ds(batch * SLOTS, SLOTS)]
        hot = (lax.broadcasted_iota(jnp.int32, (16, SLOTS), 0) == wanted).astype(F32)
        picked = jnp.dot(hot.T.astype(BF16), blocks, preferred_element_type=F32).astype(BF16)
        for w in range(WCH):
            src[batch, w] = picked[:, w * 128 : (w + 1) * 128].reshape(NS, CAP, 128)

    pl.semaphore_wait(barrier, len(LINES) + 1)

    def block_copy(q, to):
        batch, first, count = CHUNKS[q]
        cols = pl.ds(first, count)
        return pltpu.make_async_remote_copy(
            src_ref=src.at[batch, cols, to],
            dst_ref=dst.at[batch, cols, a],
            send_sem=ssem.at[q],
            recv_sem=rsem.at[q],
            device_id=(to, b),
            device_id_type=MESH,
        )

    def all_blocks(q):
        batch, first, count = CHUNKS[q]
        cols = pl.ds(first, count)
        return pltpu.make_async_remote_copy(
            src_ref=src.at[batch, cols, pl.ds(0, NS - 1)],
            dst_ref=dst.at[batch, cols, pl.ds(0, NS - 1)],
            send_sem=ssem.at[q],
            recv_sem=rsem.at[q],
            device_id=partner,
            device_id_type=MESH,
        )

    def send(q, k):
        block_copy(q, peer(k)).start()

    def send_all(peers):
        for q in range(len(CHUNKS)):
            for k in peers:
                send(q, k)

    for k in Y_LINE + Z_LINE:
        tell(near_sem, k)
    send_all(LINES)
    pl.semaphore_wait(near_sem, len(Y_LINE + Z_LINE))
    for k in Z_LINE:
        tell(wide_sem, k)
    send_all(PLANES)
    own = [
        pltpu.make_async_copy(src.at[batch, :, a], dst.at[batch, :, a], lsem.at[batch])
        for batch in range(BATCHES)
    ]
    for copy in own:
        copy.start()

    tab[...] = jnp.full(tab.shape, -1.0, F32)
    for load in loads[2:]:
        load.wait()
    for side in range(2):
        pair, place, parity = (small[3 * side + i] for i in range(3))
        tab[2 * side, :, 0:EXC] = pair.astype(F32)
        tab[2 * side + 1, :, 0:EXC] = ((1 - 2 * parity) * (place + 1)).astype(F32)
    pair_lane = lax.broadcasted_iota(jnp.int32, (EPAD, PPAD), 1).astype(F32)
    for side in range(2):
        pair_cols = tab[2 * side].T[0:EPAD]
        code_cols = tab[2 * side + 1].T[0:EPAD]
        for row in range(NV):
            hit = pair_cols[:, row : row + 1] == pair_lane
            codes[side, row] = jnp.sum(
                jnp.where(hit, code_cols[:, row : row + 1], 0.0), axis=0, keepdims=True
            )

    def signed_hot(code, count):
        place = (lax.broadcasted_iota(jnp.int32, (count, PPAD), 0) + 1).astype(F32)
        return (jnp.where(code == place, 1.0, 0.0) - jnp.where(code == -place, 1.0, 0.0)).astype(
            BF16
        )

    def beta_row(v, carry):
        tscr[pl.ds(pl.multiple_of(v * NU, NU), NU), :] = signed_hot(codes[0, v], NU)
        return carry

    lax.fori_loop(0, NV, beta_row, 0)
    ipad[...] = jnp.zeros(ipad.shape, BF16)
    ipad[0:PAIRS, 0:PAIRS] = integrals[...]
    table = jnp.dot(tscr[...], ipad[...], preferred_element_type=F32)
    high = table.astype(BF16)
    wscr[:, 0:PPAD] = high
    wscr[:, PPAD:] = (table - high.astype(F32)).astype(BF16)

    pl.semaphore_wait(wide_sem, len(Z_LINE))
    send_all(REST)

    def alpha_rows(step):
        for i in range(GSTEP):
            hot = signed_hot(codes[1, step * GSTEP + i], SLOTS)
            hots[i * SLOTS : (i + 1) * SLOTS, 0:PPAD] = hot
            hots[i * SLOTS : (i + 1) * SLOTS, PPAD:] = hot
        product = lax.dot_general(
            wscr[...], hots[...], (((1,), (1,)), ((), ())), preferred_element_type=F32
        )
        batch = step // (GB // GSTEP)
        for i in range(GSTEP):
            local = step % (GB // GSTEP) * GSTEP + i
            value = product[:, i * SLOTS : (i + 1) * SLOTS]
            top = value.astype(BF16)
            rest = (value - top.astype(F32)).astype(BF16)
            for v in range(NV):
                rows = slice(v * NU, (v + 1) * NU)
                start = (v // 2) * 2 * SLOTS
                alhs[batch, v % 2, local, :, start : start + SLOTS] = top[rows]
                alhs[batch, v % 2, local, :, start + SLOTS : start + 2 * SLOTS] = rest[rows]

    for step in range(NG // GSTEP):
        alpha_rows(step)
    swaps, keeps = [], []
    for batch in range(BATCHES):
        for h in range(2):
            place = (pl.ds(batch * GB * SB, GB * SB), pl.ds(h * 128, 128))
            swaps.append(
                pltpu.make_async_remote_copy(
                    src_ref=part.at[batch, 1 - b, h],
                    dst_ref=far_ref.at[place],
                    send_sem=psem.at[batch, h],
                    recv_sem=qsem.at[batch, h],
                    device_id=partner,
                    device_id_type=MESH,
                )
            )
            keeps.append(
                pltpu.make_async_copy(part.at[batch, b, h], own_ref.at[place], ksem.at[batch, h])
            )
    small_group = lax.broadcasted_iota(jnp.int32, (GB, 128), 1) // 16
    for batch in range(BATCHES):
        own[batch].wait()
        for q, (of_batch, first, count) in enumerate(CHUNKS):
            if of_batch != batch:
                continue
            all_blocks(q).wait_recv()
            right = []
            for w in range(first, first + count):
                right += [dst[batch, w].reshape(SLOTS, 128)] * 2
            lanes = slice(first * 2 * SLOTS, (first + count) * 2 * SLOTS)
            left = alhs[batch, :, :, :, lanes].reshape(2 * GB * NU, count * 2 * SLOTS)
            result = jnp.dot(left, jnp.concatenate(right, axis=0), preferred_element_type=F32)
            if first > 0:
                result = result + fsum[...]
            if first + count < WCH:
                fsum[...] = result
        even, odd = result[0 : GB * NU], result[GB * NU :]
        xscr[...] = even + pltpu.roll(odd, 64, 1)
        for j in range(4):
            by_u = [xscr[pl.ds(8 * j + i, GB, stride=NU), :] for i in range(8)]
            total = [jnp.zeros((GB, 128), F32) for _ in range(SB)]
            for d in range(8):
                mixed = by_u[d % 8]
                for s in range(1, SB):
                    mixed = jnp.where(small_group == s, by_u[(s + d) % 8], mixed)
                moved = pltpu.roll(mixed, 16 * d, 1) if d else mixed
                for s in range(SB):
                    total[s] = jnp.where(small_group == (s + d) % 8, moved, total[s])
            for s in range(SB):
                part.at[batch, j // 2, j % 2][pl.ds(s, GB, stride=SB), :] = total[s]
        for h in range(2):
            swaps[2 * batch + h].start()
            keeps[2 * batch + h].start()

    for q in range(len(CHUNKS)):
        all_blocks(q).wait_send()
    for swap, keep in zip(swaps, keeps):
        keep.wait()
        swap.wait()


def on_device(*operands):
    whole = pl.BlockSpec(memory_space=pl.ANY)
    own, far = pl.pallas_call(
        kernel,
        out_shape=[jax.ShapeDtypeStruct((64, 256), F32)] * 2,
        in_specs=[whole] * 9,
        out_specs=[whole] * 2,
        scratch_shapes=[
            pltpu.VMEM((64, 256), BF16),
            pltpu.VMEM((PAIRS, PAIRS), BF16),
            pltpu.VMEM((1, BATCHES * SLOTS), jnp.int32),
            pltpu.VMEM((6, 16, EXC), jnp.int32),
            pltpu.VMEM((2, 64, 128), F32),
            pltpu.VMEM((BATCHES, WCH, NS, CAP, 128), BF16),
            pltpu.VMEM((BATCHES, WCH, NS, CAP, 128), BF16),
            pltpu.VMEM((4, 16, 256), F32),
            pltpu.VMEM((2, NV, 1, PPAD), F32),
            pltpu.VMEM((NV * NU, PPAD), BF16),
            pltpu.VMEM((PPAD, PPAD), BF16),
            pltpu.VMEM((NV * NU, 2 * PPAD), BF16),
            pltpu.VMEM((BATCHES, 2, GB, NU, WCH * 2 * SLOTS), BF16),
            pltpu.VMEM((GSTEP * SLOTS, 2 * PPAD), BF16),
            pltpu.VMEM((2 * GB * NU, 128), F32),
            pltpu.VMEM((GB * NU, 128), F32),
            pltpu.VMEM((BATCHES, 2, 2, GB * SB, 128), F32),
            pltpu.SemaphoreType.REGULAR,
            pltpu.SemaphoreType.REGULAR,
            pltpu.SemaphoreType.DMA((9,)),
            pltpu.SemaphoreType.DMA((len(CHUNKS),)),
            pltpu.SemaphoreType.DMA((len(CHUNKS),)),
            pltpu.SemaphoreType.DMA((BATCHES,)),
            pltpu.SemaphoreType.DMA((BATCHES, 2)),
            pltpu.SemaphoreType.DMA((BATCHES, 2)),
            pltpu.SemaphoreType.DMA((BATCHES, 2)),
        ],
        compiler_params=pltpu.CompilerParams(
            collective_id=0, has_side_effects=True, vmem_limit_bytes=56 << 20
        ),
    )(*operands)
    return own + far


def solution(mesh):
    in_specs = (
        P("alpha", "beta"),
        P(),
        P("alpha", None),
        P("alpha", None),
        P("alpha", None),
        P("alpha", None),
        P("beta", None),
        P("beta", None),
        P("beta", None),
    )
    return jax.shard_map(
        on_device, mesh=mesh, in_specs=in_specs, out_specs=P("alpha", "beta"), check_vma=False
    )
```

```python
import functools

import jax
import jax.numpy as jnp
from jax import lax
from jax.experimental import pallas as pl
from jax.experimental.pallas import tpu as pltpu
from jax.sharding import PartitionSpec as P

MESH = pl.DeviceIdType.MESH
PAIRS = 484
PPAD = 512
EXC = 132
EPAD = 136
SB = 4
BATCHES = 2
CAP = 4
NV = 16
NU = 32
NG = 16
GB = 8
NS = 64
X_LINE, Y_LINE, Z_LINE = (1, 2, 3), (4, 8, 12), (16, 32, 48)
LINES = X_LINE + Y_LINE + Z_LINE


def dims_of(k):
    return (k % 4 > 0) + (k // 4 % 4 > 0) + (k // 16 > 0)


PLANES = tuple(k for k in range(1, 64) if dims_of(k) == 2)
REST = tuple(k for k in range(1, 64) if dims_of(k) == 3)
NEAR = LINES + PLANES
ORDER = (0,) + LINES + PLANES[:22] + REST + PLANES[22:]
POS = tuple(ORDER.index(k) for k in range(64))
CHUNKS = (
    (NEAR, 0, 0, 8),
    (NEAR, 1, 0, 8),
    (REST, 0, 0, 8),
    (REST, 1, 0, 4),
    (REST, 1, 4, 4),
)
STEPS = ((0, 0, 0), (1, 0, 1), (0, 1, 2), (1, 1, 3), (1, 1, 4))
WCH = 8
SLOTS = NS * CAP
GSTEP = 4
HALF = SLOTS // 2
F32 = jnp.float32
BF16 = jnp.bfloat16


def kernel(
    coeffs_ref,
    integrals_ref,
    send_ref,
    aslot_ref,
    apair_ref,
    apar_ref,
    bpair_ref,
    btarget_ref,
    bpar_ref,
    own_ref,
    far_ref,
    coeffs,
    integrals,
    sends,
    small,
    cscr,
    src,
    dst,
    tab,
    codes,
    tscr,
    ipad,
    wscr,
    alhs,
    hots,
    fsum,
    xscr,
    part,
    near_sem,
    wide_sem,
    insem,
    ssem,
    rsem,
    lsem,
    ksem,
    psem,
    qsem,
):
    a = lax.axis_index("alpha")
    b = lax.axis_index("beta")
    partner = (a, 1 - b)

    here = (lax.div(a, 16), lax.rem(lax.div(a, 4), 4), lax.rem(a, 4))
    steps = [[lax.rem(place + i, 4) * scale for i in range(4)] for place, scale in zip(here, (16, 4, 1))]

    def peer(k):
        return steps[0][k // 16] + (steps[1][k // 4 % 4] + steps[2][k % 4])

    barrier = pltpu.get_barrier_semaphore()
    loads = [
        pltpu.make_async_copy(ref, to, insem.at[i])
        for i, (ref, to) in enumerate(
            [(coeffs_ref, coeffs), (send_ref, sends)]
            + [
                (ref, small.at[i])
                for i, ref in enumerate(
                    [bpair_ref, btarget_ref, bpar_ref, apair_ref, aslot_ref, apar_ref]
                )
            ]
            + [(integrals_ref, integrals)]
        )
    ]
    for load in loads:
        load.start()

    def tell(semaphore, k):
        pl.semaphore_signal(semaphore, inc=1, device_id=(peer(k), b), device_id_type=MESH)

    for k in LINES:
        tell(barrier, k)
    pl.semaphore_signal(barrier, inc=1, device_id=partner, device_id_type=MESH)

    loads[0].wait()
    loads[1].wait()
    for h in range(2):
        cscr[h] = coeffs[:, h * 128 : (h + 1) * 128].astype(F32)
    lane_group = lax.broadcasted_iota(jnp.int32, (16, 128), 1) // 16
    pieces = [
        [cscr.at[h][pl.ds(s, 16, stride=SB), :] for h in range(2)] for s in range(SB)
    ]
    columns = []
    for w in range(WCH):
        value = jnp.zeros((16, 128), F32)
        for par in range(2):
            v = 2 * w + par
            for s in range(SB):
                shift = ((par * 4 + s) - (v % 8)) % 8 * 16
                piece = pieces[s][v // 8]
                moved = pltpu.roll(piece, shift, 1) if shift else piece
                value = jnp.where(lane_group == par * 4 + s, moved, value)
        columns.append(value.astype(BF16))
    blocks = jnp.concatenate(columns, axis=1)
    for batch in range(BATCHES):
        wanted = sends[:, pl.ds(batch * SLOTS, SLOTS)]
        hot = (lax.broadcasted_iota(jnp.int32, (16, SLOTS), 0) == wanted).astype(F32)
        picked = jnp.dot(hot.T.astype(BF16), blocks, preferred_element_type=F32).astype(BF16)
        for w in range(WCH):
            src[batch, w] = picked[:, w * 128 : (w + 1) * 128].reshape(NS, CAP, 128)

    pl.semaphore_wait(barrier, len(LINES) + 1)

    def block_copy(q, k):
        _, batch, first, count = CHUNKS[q]
        cols, to = pl.ds(first, count), peer(k)
        return pltpu.make_async_remote_copy(
            src_ref=src.at[batch, cols, to],
            dst_ref=dst.at[batch, cols, POS[k]],
            send_sem=ssem.at[q],
            recv_sem=rsem.at[q],
            device_id=(to, b),
            device_id_type=MESH,
        )

    def all_blocks(q):
        peers, batch, first, count = CHUNKS[q]
        cols = pl.ds(first, count)
        return pltpu.make_async_remote_copy(
            src_ref=src.at[batch, cols, pl.ds(0, len(peers))],
            dst_ref=dst.at[batch, cols, pl.ds(0, len(peers))],
            send_sem=ssem.at[q],
            recv_sem=rsem.at[q],
            device_id=partner,
            device_id_type=MESH,
        )

    def send(q, k):
        block_copy(q, k).start()

    def send_all(peers):
        for q, chunk in enumerate(CHUNKS):
            for k in peers:
                if k in chunk[0]:
                    send(q, k)

    for k in Y_LINE + Z_LINE:
        tell(near_sem, k)
    send_all(LINES)
    pl.semaphore_wait(near_sem, len(Y_LINE + Z_LINE))
    for k in Z_LINE:
        tell(wide_sem, k)
    send_all(PLANES)
    own = [
        pltpu.make_async_copy(src.at[batch, :, a], dst.at[batch, :, POS[0]], lsem.at[batch])
        for batch in range(BATCHES)
    ]
    for copy in own:
        copy.start()

    tab[...] = jnp.full(tab.shape, -1.0, F32)
    for load in loads[2:]:
        load.wait()
    for side in range(2):
        pair, place, parity = (small[3 * side + i] for i in range(3))
        if side == 1:
            sender = lax.shift_right_logical(place, 2)
            apart = (
                ((here[0] - lax.shift_right_logical(sender, 4)) & 3) * 16
                + ((here[1] - (lax.shift_right_logical(sender, 2) & 3)) & 3) * 4
                + ((here[2] - (sender & 3)) & 3)
            )
            slot = place & 3
            for k in range(NS):
                slot = slot + jnp.where(apart == k, POS[k] * CAP, 0)
            place = slot
        tab[2 * side, :, 0:EXC] = pair.astype(F32)
        tab[2 * side + 1, :, 0:EXC] = ((1 - 2 * parity) * (place + 1)).astype(F32)
    pair_lane = lax.broadcasted_iota(jnp.int32, (EPAD, PPAD), 1).astype(F32)
    for side in range(2):
        pair_cols = tab[2 * side].T[0:EPAD]
        code_cols = tab[2 * side + 1].T[0:EPAD]
        for row in range(NV):
            hit = pair_cols[:, row : row + 1] == pair_lane
            codes[side, row] = jnp.sum(
                jnp.where(hit, code_cols[:, row : row + 1], 0.0), axis=0, keepdims=True
            )

    def signed_hot(code, count):
        place = (lax.broadcasted_iota(jnp.int32, (count, PPAD), 0) + 1).astype(F32)
        return (jnp.where(code == place, 1.0, 0.0) - jnp.where(code == -place, 1.0, 0.0)).astype(
            BF16
        )

    def beta_row(v, carry):
        tscr[pl.ds(pl.multiple_of(v * NU, NU), NU), :] = signed_hot(codes[0, v], NU)
        return carry

    lax.fori_loop(0, NV, beta_row, 0)
    ipad[...] = jnp.zeros(ipad.shape, BF16)
    ipad[0:PAIRS, 0:PAIRS] = integrals[...]
    table = jnp.dot(tscr[...], ipad[...], preferred_element_type=F32)
    high = table.astype(BF16)
    wscr[:, 0:PPAD] = high
    wscr[:, PPAD:] = (table - high.astype(F32)).astype(BF16)

    pl.semaphore_wait(wide_sem, len(Z_LINE))
    send_all(REST)

    def alpha_rows(step):
        for i in range(GSTEP):
            hot = signed_hot(codes[1, step * GSTEP + i], SLOTS)
            hots[i * SLOTS : (i + 1) * SLOTS, 0:PPAD] = hot
            hots[i * SLOTS : (i + 1) * SLOTS, PPAD:] = hot
        product = lax.dot_general(
            wscr[...], hots[...], (((1,), (1,)), ((), ())), preferred_element_type=F32
        )
        batch = step // (GB // GSTEP)
        for i in range(GSTEP):
            local = step % (GB // GSTEP) * GSTEP + i
            value = product[:, i * SLOTS : (i + 1) * SLOTS]
            top = value.astype(BF16)
            rest = (value - top.astype(F32)).astype(BF16)
            for v in range(NV):
                rows = slice(v * NU, (v + 1) * NU)
                for half in range(2):
                    start = half * WCH * SLOTS + (v // 2) * SLOTS
                    lanes = slice(half * HALF, (half + 1) * HALF)
                    alhs[batch, v % 2, local, :, start : start + HALF] = top[rows, lanes]
                    alhs[batch, v % 2, local, :, start + HALF : start + SLOTS] = rest[rows, lanes]

    for step in range(NG // GSTEP):
        alpha_rows(step)
    swaps, keeps = [], []
    for batch in range(BATCHES):
        for h in range(2):
            place = (pl.ds(batch * GB * SB, GB * SB), pl.ds(h * 128, 128))
            swaps.append(
                pltpu.make_async_remote_copy(
                    src_ref=part.at[batch, 1 - b, h],
                    dst_ref=far_ref.at[place],
                    send_sem=psem.at[batch, h],
                    recv_sem=qsem.at[batch, h],
                    device_id=partner,
                    device_id_type=MESH,
                )
            )
            keeps.append(
                pltpu.make_async_copy(part.at[batch, b, h], own_ref.at[place], ksem.at[batch, h])
            )
    small_group = lax.broadcasted_iota(jnp.int32, (GB, 128), 1) // 16
    for batch, half, q in STEPS:
        _, _, first, count = CHUNKS[q]
        if half == 0:
            own[batch].wait()
        all_blocks(q).wait_recv()
        right = []
        for w in range(first, first + count):
            right += [dst[batch, w, half * NS // 2 : (half + 1) * NS // 2].reshape(HALF, 128)] * 2
        start = half * WCH * SLOTS + first * SLOTS
        left = alhs[batch, :, :, :, start : start + count * SLOTS]
        result = jnp.dot(
            left.reshape(2 * GB * NU, count * SLOTS),
            jnp.concatenate(right, axis=0),
            preferred_element_type=F32,
        )
        if half == 1:
            result = result + fsum[batch]
        if half == 0 or first + count < WCH:
            fsum[batch] = result
            continue
        even, odd = result[0 : GB * NU], result[GB * NU :]
        xscr[...] = even + pltpu.roll(odd, 64, 1)
        for j in range(4):
            by_u = [xscr[pl.ds(8 * j + i, GB, stride=NU), :] for i in range(8)]
            total = [jnp.zeros((GB, 128), F32) for _ in range(SB)]
            for d in range(8):
                mixed = by_u[d % 8]
                for s in range(1, SB):
                    mixed = jnp.where(small_group == s, by_u[(s + d) % 8], mixed)
                moved = pltpu.roll(mixed, 16 * d, 1) if d else mixed
                for s in range(SB):
                    total[s] = jnp.where(small_group == (s + d) % 8, moved, total[s])
            for s in range(SB):
                part.at[batch, j // 2, j % 2][pl.ds(s, GB, stride=SB), :] = total[s]
        for h in range(2):
            swaps[2 * batch + h].start()
            keeps[2 * batch + h].start()

    for q in range(len(CHUNKS)):
        all_blocks(q).wait_send()
    for swap, keep in zip(swaps, keeps):
        keep.wait()
        swap.wait()


def on_device(*operands):
    whole = pl.BlockSpec(memory_space=pl.ANY)
    own, far = pl.pallas_call(
        kernel,
        out_shape=[jax.ShapeDtypeStruct((64, 256), F32)] * 2,
        in_specs=[pl.BlockSpec(memory_space=pltpu.HBM)] * 9,
        out_specs=[pl.BlockSpec(memory_space=pltpu.VMEM)] * 2,
        scratch_shapes=[
            pltpu.VMEM((64, 256), BF16),
            pltpu.VMEM((PAIRS, PAIRS), BF16),
            pltpu.VMEM((1, BATCHES * SLOTS), jnp.int32),
            pltpu.VMEM((6, 16, EXC), jnp.int32),
            pltpu.VMEM((2, 64, 128), F32),
            pltpu.VMEM((BATCHES, WCH, NS, CAP, 128), BF16),
            pltpu.VMEM((BATCHES, WCH, NS, CAP, 128), BF16),
            pltpu.VMEM((4, 16, 256), F32),
            pltpu.VMEM((2, NV, 1, PPAD), F32),
            pltpu.VMEM((NV * NU, PPAD), BF16),
            pltpu.VMEM((PPAD, PPAD), BF16),
            pltpu.VMEM((NV * NU, 2 * PPAD), BF16),
            pltpu.VMEM((BATCHES, 2, GB, NU, WCH * 2 * SLOTS), BF16),
            pltpu.VMEM((GSTEP * SLOTS, 2 * PPAD), BF16),
            pltpu.VMEM((BATCHES, 2 * GB * NU, 128), F32),
            pltpu.VMEM((GB * NU, 128), F32),
            pltpu.VMEM((BATCHES, 2, 2, GB * SB, 128), F32),
            pltpu.SemaphoreType.REGULAR,
            pltpu.SemaphoreType.REGULAR,
            pltpu.SemaphoreType.DMA((9,)),
            pltpu.SemaphoreType.DMA((len(CHUNKS),)),
            pltpu.SemaphoreType.DMA((len(CHUNKS),)),
            pltpu.SemaphoreType.DMA((BATCHES,)),
            pltpu.SemaphoreType.DMA((BATCHES, 2)),
            pltpu.SemaphoreType.DMA((BATCHES, 2)),
            pltpu.SemaphoreType.DMA((BATCHES, 2)),
        ],
        compiler_params=pltpu.CompilerParams(
            collective_id=0, has_side_effects=True, vmem_limit_bytes=28 << 20
        ),
    )(*[pltpu.with_memory_space_constraint(x, pltpu.HBM) for x in operands])
    return own + far


def solution(mesh):
    in_specs = (
        P("alpha", "beta"),
        P(),
        P("alpha", None),
        P("alpha", None),
        P("alpha", None),
        P("alpha", None),
        P("beta", None),
        P("beta", None),
        P("beta", None),
    )
    return jax.shard_map(
        on_device, mesh=mesh, in_specs=in_specs, out_specs=P("alpha", "beta"), check_vma=False
    )
```

```python
import functools

import jax
import jax.numpy as jnp
from jax import lax
from jax.experimental import pallas as pl
from jax.experimental.pallas import tpu as pltpu
from jax.sharding import PartitionSpec as P

MESH = pl.DeviceIdType.MESH
PAIRS = 484
PPAD = 512
EXC = 132
EPAD = 136
SB = 4
BATCHES = 2
CAP = 4
NV = 16
NU = 32
NG = 16
GB = 8
NS = 64
X_LINE, Y_LINE, Z_LINE = (1, 2, 3), (4, 8, 12), (16, 32, 48)
LINES = X_LINE + Y_LINE + Z_LINE


def dims_of(k):
    return (k % 4 > 0) + (k // 4 % 4 > 0) + (k // 16 > 0)


PLANES = tuple(k for k in range(1, 64) if dims_of(k) == 2)
REST = tuple(k for k in range(1, 64) if dims_of(k) == 3)
NEAR = LINES + PLANES


def first_leg(k):
    digits = (k % 4, k // 4 % 4 * 4, k // 16 * 16)
    return digits[sum((k % 4, k // 4 % 4, k // 16)) % 3]


ORDER = (0,) + LINES + PLANES[:22] + REST + PLANES[22:]
POS = tuple(ORDER.index(k) for k in range(64))
CHUNKS = (
    (NEAR, 0, 0, 8),
    (NEAR, 1, 0, 8),
    (REST, 0, 0, 8),
    (REST, 1, 0, 4),
    (REST, 1, 4, 4),
)
STEPS = ((0, 0, 0), (1, 0, 1), (0, 1, 2), (1, 1, 3), (1, 1, 4))
WCH = 8
SLOTS = NS * CAP
GSTEP = 4
HALF = SLOTS // 2
F32 = jnp.float32
BF16 = jnp.bfloat16


def kernel(
    coeffs_ref,
    integrals_ref,
    send_ref,
    aslot_ref,
    apair_ref,
    apar_ref,
    bpair_ref,
    btarget_ref,
    bpar_ref,
    own_ref,
    far_ref,
    coeffs,
    integrals,
    sends,
    small,
    cscr,
    src,
    dst,
    tab,
    codes,
    tscr,
    ipad,
    wscr,
    alhs,
    transit,
    hots,
    fsum,
    xscr,
    part,
    near_sem,
    tsend,
    trecv,
    insem,
    ssem,
    rsem,
    lsem,
    ksem,
    psem,
    qsem,
):
    a = lax.axis_index("alpha")
    b = lax.axis_index("beta")
    partner = (a, 1 - b)

    here = (lax.div(a, 16), lax.rem(lax.div(a, 4), 4), lax.rem(a, 4))
    steps = [[lax.rem(place + i, 4) * scale for i in range(4)] for place, scale in zip(here, (16, 4, 1))]

    def peer(k):
        return steps[0][k // 16] + (steps[1][k // 4 % 4] + steps[2][k % 4])

    barrier = pltpu.get_barrier_semaphore()
    loads = [
        pltpu.make_async_copy(ref, to, insem.at[i])
        for i, (ref, to) in enumerate(
            [(coeffs_ref, coeffs), (send_ref, sends)]
            + [
                (ref, small.at[i])
                for i, ref in enumerate(
                    [bpair_ref, btarget_ref, bpar_ref, apair_ref, aslot_ref, apar_ref]
                )
            ]
            + [(integrals_ref, integrals)]
        )
    ]
    for load in loads:
        load.start()

    def tell(semaphore, k):
        pl.semaphore_signal(semaphore, inc=1, device_id=(peer(k), b), device_id_type=MESH)

    for k in LINES:
        tell(barrier, k)
    pl.semaphore_signal(barrier, inc=1, device_id=partner, device_id_type=MESH)

    loads[0].wait()
    loads[1].wait()
    for h in range(2):
        cscr[h] = coeffs[:, h * 128 : (h + 1) * 128].astype(F32)
    lane_group = lax.broadcasted_iota(jnp.int32, (16, 128), 1) // 16
    pieces = [
        [cscr.at[h][pl.ds(s, 16, stride=SB), :] for h in range(2)] for s in range(SB)
    ]
    columns = []
    for w in range(WCH):
        value = jnp.zeros((16, 128), F32)
        for par in range(2):
            v = 2 * w + par
            for s in range(SB):
                shift = ((par * 4 + s) - (v % 8)) % 8 * 16
                piece = pieces[s][v // 8]
                moved = pltpu.roll(piece, shift, 1) if shift else piece
                value = jnp.where(lane_group == par * 4 + s, moved, value)
        columns.append(value.astype(BF16))
    blocks = jnp.concatenate(columns, axis=1)
    for batch in range(BATCHES):
        wanted = sends[:, pl.ds(batch * SLOTS, SLOTS)]
        hot = (lax.broadcasted_iota(jnp.int32, (16, SLOTS), 0) == wanted).astype(F32)
        picked = jnp.dot(hot.T.astype(BF16), blocks, preferred_element_type=F32).astype(BF16)
        for w in range(WCH):
            src[batch, w] = picked[:, w * 128 : (w + 1) * 128].reshape(NS, CAP, 128)

    pl.semaphore_wait(barrier, len(LINES) + 1)

    def first_copy(batch, i):
        to, relay = peer(REST[i]), peer(first_leg(REST[i]))
        return pltpu.make_async_remote_copy(
            src_ref=src.at[batch, :, to],
            dst_ref=transit.at[batch, :, i],
            send_sem=tsend.at[batch],
            recv_sem=trecv.at[batch],
            device_id=(relay, b),
            device_id_type=MESH,
        )

    def in_transit(batch):
        return pltpu.make_async_remote_copy(
            src_ref=src.at[batch, :, pl.ds(0, len(REST))],
            dst_ref=transit.at[batch],
            send_sem=tsend.at[batch],
            recv_sem=trecv.at[batch],
            device_id=partner,
            device_id_type=MESH,
        )

    def forward(q, i):
        _, batch, first, count = CHUNKS[q]
        cols, k = pl.ds(first, count), REST[i]
        return pltpu.make_async_remote_copy(
            src_ref=transit.at[batch, cols, i],
            dst_ref=dst.at[batch, cols, POS[k]],
            send_sem=ssem.at[q],
            recv_sem=rsem.at[q],
            device_id=(peer(k - first_leg(k)), b),
            device_id_type=MESH,
        )

    def block_copy(q, k):
        _, batch, first, count = CHUNKS[q]
        cols, to = pl.ds(first, count), peer(k)
        return pltpu.make_async_remote_copy(
            src_ref=src.at[batch, cols, to],
            dst_ref=dst.at[batch, cols, POS[k]],
            send_sem=ssem.at[q],
            recv_sem=rsem.at[q],
            device_id=(to, b),
            device_id_type=MESH,
        )

    def all_blocks(q):
        peers, batch, first, count = CHUNKS[q]
        cols = pl.ds(first, count)
        return pltpu.make_async_remote_copy(
            src_ref=src.at[batch, cols, pl.ds(0, len(peers))],
            dst_ref=dst.at[batch, cols, pl.ds(0, len(peers))],
            send_sem=ssem.at[q],
            recv_sem=rsem.at[q],
            device_id=partner,
            device_id_type=MESH,
        )

    def send(q, k):
        block_copy(q, k).start()

    def send_all(peers):
        for q, chunk in enumerate(CHUNKS):
            for k in peers:
                if k in chunk[0]:
                    send(q, k)

    for k in Y_LINE + Z_LINE:
        tell(near_sem, k)
    for batch in range(BATCHES):
        for i in range(len(REST)):
            first_copy(batch, i).start()
    send_all(LINES)
    own = [
        pltpu.make_async_copy(src.at[batch, :, a], dst.at[batch, :, POS[0]], lsem.at[batch])
        for batch in range(BATCHES)
    ]
    for copy in own:
        copy.start()

    tab[...] = jnp.full(tab.shape, -1.0, F32)
    for load in loads[2:]:
        load.wait()
    for side in range(2):
        pair, place, parity = (small[3 * side + i] for i in range(3))
        if side == 1:
            sender = lax.shift_right_logical(place, 2)
            apart = (
                ((here[0] - lax.shift_right_logical(sender, 4)) & 3) * 16
                + ((here[1] - (lax.shift_right_logical(sender, 2) & 3)) & 3) * 4
                + ((here[2] - (sender & 3)) & 3)
            )
            slot = place & 3
            for k in range(NS):
                slot = slot + jnp.where(apart == k, POS[k] * CAP, 0)
            place = slot
        tab[2 * side, :, 0:EXC] = pair.astype(F32)
        tab[2 * side + 1, :, 0:EXC] = ((1 - 2 * parity) * (place + 1)).astype(F32)
    pair_lane = lax.broadcasted_iota(jnp.int32, (EPAD, PPAD), 1).astype(F32)
    for side in range(2):
        pair_cols = tab[2 * side].T[0:EPAD]
        code_cols = tab[2 * side + 1].T[0:EPAD]
        for row in range(NV):
            hit = pair_cols[:, row : row + 1] == pair_lane
            codes[side, row] = jnp.sum(
                jnp.where(hit, code_cols[:, row : row + 1], 0.0), axis=0, keepdims=True
            )

    def signed_hot(code, count):
        place = (lax.broadcasted_iota(jnp.int32, (count, PPAD), 0) + 1).astype(F32)
        return (jnp.where(code == place, 1.0, 0.0) - jnp.where(code == -place, 1.0, 0.0)).astype(
            BF16
        )

    def beta_row(v, carry):
        tscr[pl.ds(pl.multiple_of(v * NU, NU), NU), :] = signed_hot(codes[0, v], NU)
        return carry

    lax.fori_loop(0, NV, beta_row, 0)
    ipad[...] = jnp.zeros(ipad.shape, BF16)
    ipad[0:PAIRS, 0:PAIRS] = integrals[...]
    table = jnp.dot(tscr[...], ipad[...], preferred_element_type=F32)
    high = table.astype(BF16)
    wscr[:, 0:PPAD] = high
    wscr[:, PPAD:] = (table - high.astype(F32)).astype(BF16)

    pl.semaphore_wait(near_sem, len(Y_LINE + Z_LINE))
    send_all(PLANES)
    for batch in range(BATCHES):
        in_transit(batch).wait_recv()
        for q, chunk in enumerate(CHUNKS):
            if chunk[0] == REST and chunk[1] == batch:
                for i in range(len(REST)):
                    forward(q, i).start()

    def alpha_rows(step):
        for i in range(GSTEP):
            hot = signed_hot(codes[1, step * GSTEP + i], SLOTS)
            hots[i * SLOTS : (i + 1) * SLOTS, 0:PPAD] = hot
            hots[i * SLOTS : (i + 1) * SLOTS, PPAD:] = hot
        product = lax.dot_general(
            wscr[...], hots[...], (((1,), (1,)), ((), ())), preferred_element_type=F32
        )
        batch = step // (GB // GSTEP)
        for i in range(GSTEP):
            local = step % (GB // GSTEP) * GSTEP + i
            value = product[:, i * SLOTS : (i + 1) * SLOTS]
            top = value.astype(BF16)
            rest = (value - top.astype(F32)).astype(BF16)
            for v in range(NV):
                rows = slice(v * NU, (v + 1) * NU)
                for half in range(2):
                    start = half * WCH * SLOTS + (v // 2) * SLOTS
                    lanes = slice(half * HALF, (half + 1) * HALF)
                    alhs[batch, v % 2, local, :, start : start + HALF] = top[rows, lanes]
                    alhs[batch, v % 2, local, :, start + HALF : start + SLOTS] = rest[rows, lanes]

    for step in range(NG // GSTEP):
        alpha_rows(step)
    swaps, keeps = [], []
    for batch in range(BATCHES):
        for h in range(2):
            place = (pl.ds(batch * GB * SB, GB * SB), pl.ds(h * 128, 128))
            swaps.append(
                pltpu.make_async_remote_copy(
                    src_ref=part.at[batch, 1 - b, h],
                    dst_ref=far_ref.at[place],
                    send_sem=psem.at[batch, h],
                    recv_sem=qsem.at[batch, h],
                    device_id=partner,
                    device_id_type=MESH,
                )
            )
            keeps.append(
                pltpu.make_async_copy(part.at[batch, b, h], own_ref.at[place], ksem.at[batch, h])
            )
    small_group = lax.broadcasted_iota(jnp.int32, (GB, 128), 1) // 16
    for batch, half, q in STEPS:
        _, _, first, count = CHUNKS[q]
        if half == 0:
            own[batch].wait()
        all_blocks(q).wait_recv()
        right = []
        for w in range(first, first + count):
            right += [dst[batch, w, half * NS // 2 : (half + 1) * NS // 2].reshape(HALF, 128)] * 2
        start = half * WCH * SLOTS + first * SLOTS
        left = alhs[batch, :, :, :, start : start + count * SLOTS]
        result = jnp.dot(
            left.reshape(2 * GB * NU, count * SLOTS),
            jnp.concatenate(right, axis=0),
            preferred_element_type=F32,
        )
        if half == 1:
            result = result + fsum[batch]
        if half == 0 or first + count < WCH:
            fsum[batch] = result
            continue
        even, odd = result[0 : GB * NU], result[GB * NU :]
        xscr[...] = even + pltpu.roll(odd, 64, 1)
        for j in range(4):
            by_u = [xscr[pl.ds(8 * j + i, GB, stride=NU), :] for i in range(8)]
            total = [jnp.zeros((GB, 128), F32) for _ in range(SB)]
            for d in range(8):
                mixed = by_u[d % 8]
                for s in range(1, SB):
                    mixed = jnp.where(small_group == s, by_u[(s + d) % 8], mixed)
                moved = pltpu.roll(mixed, 16 * d, 1) if d else mixed
                for s in range(SB):
                    total[s] = jnp.where(small_group == (s + d) % 8, moved, total[s])
            for s in range(SB):
                part.at[batch, j // 2, j % 2][pl.ds(s, GB, stride=SB), :] = total[s]
        for h in range(2):
            swaps[2 * batch + h].start()
            keeps[2 * batch + h].start()

    for batch in range(BATCHES):
        in_transit(batch).wait_send()
    for q in range(len(CHUNKS)):
        all_blocks(q).wait_send()
    for swap, keep in zip(swaps, keeps):
        keep.wait()
        swap.wait()


def on_device(*operands):
    whole = pl.BlockSpec(memory_space=pl.ANY)
    own, far = pl.pallas_call(
        kernel,
        out_shape=[jax.ShapeDtypeStruct((64, 256), F32)] * 2,
        in_specs=[pl.BlockSpec(memory_space=pltpu.HBM)] * 9,
        out_specs=[pl.BlockSpec(memory_space=pltpu.VMEM)] * 2,
        scratch_shapes=[
            pltpu.VMEM((64, 256), BF16),
            pltpu.VMEM((PAIRS, PAIRS), BF16),
            pltpu.VMEM((1, BATCHES * SLOTS), jnp.int32),
            pltpu.VMEM((6, 16, EXC), jnp.int32),
            pltpu.VMEM((2, 64, 128), F32),
            pltpu.VMEM((BATCHES, WCH, NS, CAP, 128), BF16),
            pltpu.VMEM((BATCHES, WCH, NS, CAP, 128), BF16),
            pltpu.VMEM((4, 16, 256), F32),
            pltpu.VMEM((2, NV, 1, PPAD), F32),
            pltpu.VMEM((NV * NU, PPAD), BF16),
            pltpu.VMEM((PPAD, PPAD), BF16),
            pltpu.VMEM((NV * NU, 2 * PPAD), BF16),
            pltpu.VMEM((BATCHES, 2, GB, NU, WCH * 2 * SLOTS), BF16),
            pltpu.VMEM((BATCHES, WCH, len(REST), CAP, 128), BF16),
            pltpu.VMEM((GSTEP * SLOTS, 2 * PPAD), BF16),
            pltpu.VMEM((BATCHES, 2 * GB * NU, 128), F32),
            pltpu.VMEM((GB * NU, 128), F32),
            pltpu.VMEM((BATCHES, 2, 2, GB * SB, 128), F32),
            pltpu.SemaphoreType.REGULAR,
            pltpu.SemaphoreType.DMA((BATCHES,)),
            pltpu.SemaphoreType.DMA((BATCHES,)),
            pltpu.SemaphoreType.DMA((9,)),
            pltpu.SemaphoreType.DMA((len(CHUNKS),)),
            pltpu.SemaphoreType.DMA((len(CHUNKS),)),
            pltpu.SemaphoreType.DMA((BATCHES,)),
            pltpu.SemaphoreType.DMA((BATCHES, 2)),
            pltpu.SemaphoreType.DMA((BATCHES, 2)),
            pltpu.SemaphoreType.DMA((BATCHES, 2)),
        ],
        compiler_params=pltpu.CompilerParams(
            collective_id=0, has_side_effects=True, vmem_limit_bytes=28 << 20
        ),
    )(*[pltpu.with_memory_space_constraint(x, pltpu.HBM) for x in operands])
    return own + far


def solution(mesh):
    in_specs = (
        P("alpha", "beta"),
        P(),
        P("alpha", None),
        P("alpha", None),
        P("alpha", None),
        P("alpha", None),
        P("beta", None),
        P("beta", None),
        P("beta", None),
    )
    return jax.shard_map(
        on_device, mesh=mesh, in_specs=in_specs, out_specs=P("alpha", "beta"), check_vma=False
    )
```

```python
import functools

import jax
import jax.numpy as jnp
from jax import lax
from jax.experimental import pallas as pl
from jax.experimental.pallas import tpu as pltpu
from jax.sharding import PartitionSpec as P

MESH = pl.DeviceIdType.MESH
PAIRS = 484
PPAD = 512
EXC = 132
EPAD = 136
SB = 4
BATCHES = 2
CAP = 4
NV = 16
NU = 32
NG = 16
GB = 8
NS = 64
X_LINE, Y_LINE, Z_LINE = (1, 2, 3), (4, 8, 12), (16, 32, 48)
LINES = X_LINE + Y_LINE + Z_LINE


def dims_of(k):
    return (k % 4 > 0) + (k // 4 % 4 > 0) + (k // 16 > 0)


PLANES = tuple(k for k in range(1, 64) if dims_of(k) == 2)
REST = tuple(k for k in range(1, 64) if dims_of(k) == 3)
NEAR = LINES + PLANES


def first_leg(k):
    digits = (k % 4, k // 4 % 4 * 4, k // 16 * 16)
    return digits[sum((k % 4, k // 4 % 4, k // 16)) % 3]


ORDER = (0,) + LINES + PLANES[:22] + REST + PLANES[22:]
POS = tuple(ORDER.index(k) for k in range(64))
CHUNKS = (
    (NEAR, 0, 0, 8),
    (NEAR, 1, 0, 8),
    (REST, 0, 0, 8),
    (REST, 1, 0, 4),
    (REST, 1, 4, 4),
)
STEPS = ((0, 0, 0), (0, 1, 2), (1, 0, 1), (1, 1, 3), (1, 1, 4))
WCH = 8
SLOTS = NS * CAP
GSTEP = 4
HALF = SLOTS // 2
F32 = jnp.float32
BF16 = jnp.bfloat16


def kernel(
    coeffs_ref,
    integrals_ref,
    send_ref,
    aslot_ref,
    apair_ref,
    apar_ref,
    bpair_ref,
    btarget_ref,
    bpar_ref,
    own_ref,
    far_ref,
    coeffs,
    integrals,
    sends,
    small,
    cscr,
    src,
    dst,
    tab,
    codes,
    tscr,
    ipad,
    wscr,
    alhs,
    transit,
    hots,
    fsum,
    xscr,
    part,
    near_sem,
    tsend,
    trecv,
    insem,
    ssem,
    rsem,
    lsem,
    ksem,
    psem,
    qsem,
):
    a = lax.axis_index("alpha")
    b = lax.axis_index("beta")
    partner = (a, 1 - b)

    here = (lax.div(a, 16), lax.rem(lax.div(a, 4), 4), lax.rem(a, 4))
    steps = [[lax.rem(place + i, 4) * scale for i in range(4)] for place, scale in zip(here, (16, 4, 1))]

    def peer(k):
        return steps[0][k // 16] + (steps[1][k // 4 % 4] + steps[2][k % 4])

    barrier = pltpu.get_barrier_semaphore()
    loads = [
        pltpu.make_async_copy(ref, to, insem.at[i])
        for i, (ref, to) in enumerate(
            [(coeffs_ref, coeffs), (send_ref, sends)]
            + [
                (ref, small.at[i])
                for i, ref in enumerate(
                    [bpair_ref, btarget_ref, bpar_ref, apair_ref, aslot_ref, apar_ref]
                )
            ]
            + [(integrals_ref, integrals)]
        )
    ]
    for load in loads:
        load.start()

    def tell(semaphore, k):
        pl.semaphore_signal(semaphore, inc=1, device_id=(peer(k), b), device_id_type=MESH)

    for k in LINES:
        tell(barrier, k)
    pl.semaphore_signal(barrier, inc=1, device_id=partner, device_id_type=MESH)

    loads[0].wait()
    loads[1].wait()
    for h in range(2):
        cscr[h] = coeffs[:, h * 128 : (h + 1) * 128].astype(F32)
    lane_group = lax.broadcasted_iota(jnp.int32, (16, 128), 1) // 16
    pieces = [
        [cscr.at[h][pl.ds(s, 16, stride=SB), :] for h in range(2)] for s in range(SB)
    ]
    columns = []
    for w in range(WCH):
        value = jnp.zeros((16, 128), F32)
        for par in range(2):
            v = 2 * w + par
            for s in range(SB):
                shift = ((par * 4 + s) - (v % 8)) % 8 * 16
                piece = pieces[s][v // 8]
                moved = pltpu.roll(piece, shift, 1) if shift else piece
                value = jnp.where(lane_group == par * 4 + s, moved, value)
        columns.append(value.astype(BF16))
    blocks = jnp.concatenate(columns, axis=1)
    for batch in range(BATCHES):
        wanted = sends[:, pl.ds(batch * SLOTS, SLOTS)]
        hot = (lax.broadcasted_iota(jnp.int32, (16, SLOTS), 0) == wanted).astype(F32)
        picked = jnp.dot(hot.T.astype(BF16), blocks, preferred_element_type=F32).astype(BF16)
        for w in range(WCH):
            src[batch, w] = picked[:, w * 128 : (w + 1) * 128].reshape(NS, CAP, 128)

    pl.semaphore_wait(barrier, len(LINES) + 1)

    def first_copy(batch, i):
        to, relay = peer(REST[i]), peer(first_leg(REST[i]))
        return pltpu.make_async_remote_copy(
            src_ref=src.at[batch, :, to],
            dst_ref=transit.at[batch, :, i],
            send_sem=tsend.at[batch],
            recv_sem=trecv.at[batch],
            device_id=(relay, b),
            device_id_type=MESH,
        )

    def in_transit(batch):
        return pltpu.make_async_remote_copy(
            src_ref=src.at[batch, :, pl.ds(0, len(REST))],
            dst_ref=transit.at[batch],
            send_sem=tsend.at[batch],
            recv_sem=trecv.at[batch],
            device_id=partner,
            device_id_type=MESH,
        )

    def forward(q, i):
        _, batch, first, count = CHUNKS[q]
        cols, k = pl.ds(first, count), REST[i]
        return pltpu.make_async_remote_copy(
            src_ref=transit.at[batch, cols, i],
            dst_ref=dst.at[batch, cols, POS[k]],
            send_sem=ssem.at[q],
            recv_sem=rsem.at[q],
            device_id=(peer(k - first_leg(k)), b),
            device_id_type=MESH,
        )

    def block_copy(q, k):
        _, batch, first, count = CHUNKS[q]
        cols, to = pl.ds(first, count), peer(k)
        return pltpu.make_async_remote_copy(
            src_ref=src.at[batch, cols, to],
            dst_ref=dst.at[batch, cols, POS[k]],
            send_sem=ssem.at[q],
            recv_sem=rsem.at[q],
            device_id=(to, b),
            device_id_type=MESH,
        )

    def all_blocks(q):
        peers, batch, first, count = CHUNKS[q]
        cols = pl.ds(first, count)
        return pltpu.make_async_remote_copy(
            src_ref=src.at[batch, cols, pl.ds(0, len(peers))],
            dst_ref=dst.at[batch, cols, pl.ds(0, len(peers))],
            send_sem=ssem.at[q],
            recv_sem=rsem.at[q],
            device_id=partner,
            device_id_type=MESH,
        )

    def send(q, k):
        block_copy(q, k).start()

    def send_all(peers):
        for q, chunk in enumerate(CHUNKS):
            for k in peers:
                if k in chunk[0]:
                    send(q, k)

    for k in Y_LINE + Z_LINE:
        tell(near_sem, k)
    for batch in range(BATCHES):
        for i in range(len(REST)):
            first_copy(batch, i).start()
    send_all(LINES)
    own = [
        pltpu.make_async_copy(src.at[batch, :, a], dst.at[batch, :, POS[0]], lsem.at[batch])
        for batch in range(BATCHES)
    ]
    for copy in own:
        copy.start()

    tab[...] = jnp.full(tab.shape, -1.0, F32)
    for load in loads[2:]:
        load.wait()
    for side in range(2):
        pair, place, parity = (small[3 * side + i] for i in range(3))
        if side == 1:
            sender = lax.shift_right_logical(place, 2)
            apart = (
                ((here[0] - lax.shift_right_logical(sender, 4)) & 3) * 16
                + ((here[1] - (lax.shift_right_logical(sender, 2) & 3)) & 3) * 4
                + ((here[2] - (sender & 3)) & 3)
            )
            slot = place & 3
            for k in range(NS):
                slot = slot + jnp.where(apart == k, POS[k] * CAP, 0)
            place = slot
        tab[2 * side, :, 0:EXC] = pair.astype(F32)
        tab[2 * side + 1, :, 0:EXC] = ((1 - 2 * parity) * (place + 1)).astype(F32)
    pair_lane = lax.broadcasted_iota(jnp.int32, (EPAD, PPAD), 1).astype(F32)
    for side in range(2):
        pair_cols = tab[2 * side].T[0:EPAD]
        code_cols = tab[2 * side + 1].T[0:EPAD]
        for row in range(NV):
            hit = pair_cols[:, row : row + 1] == pair_lane
            codes[side, row] = jnp.sum(
                jnp.where(hit, code_cols[:, row : row + 1], 0.0), axis=0, keepdims=True
            )

    def signed_hot(code, count):
        place = (lax.broadcasted_iota(jnp.int32, (count, PPAD), 0) + 1).astype(F32)
        return (jnp.where(code == place, 1.0, 0.0) - jnp.where(code == -place, 1.0, 0.0)).astype(
            BF16
        )

    def beta_row(v, carry):
        tscr[pl.ds(pl.multiple_of(v * NU, NU), NU), :] = signed_hot(codes[0, v], NU)
        return carry

    lax.fori_loop(0, NV, beta_row, 0)
    ipad[...] = jnp.zeros(ipad.shape, BF16)
    ipad[0:PAIRS, 0:PAIRS] = integrals[...]
    table = jnp.dot(tscr[...], ipad[...], preferred_element_type=F32)
    high = table.astype(BF16)
    wscr[:, 0:PPAD] = high
    wscr[:, PPAD:] = (table - high.astype(F32)).astype(BF16)

    pl.semaphore_wait(near_sem, len(Y_LINE + Z_LINE))
    for batch in range(BATCHES):
        for k in PLANES:
            send(batch, k)
        in_transit(batch).wait_recv()
        for q, chunk in enumerate(CHUNKS):
            if chunk[0] == REST and chunk[1] == batch:
                for i in range(len(REST)):
                    forward(q, i).start()

    def alpha_rows(step):
        for i in range(GSTEP):
            hot = signed_hot(codes[1, step * GSTEP + i], SLOTS)
            hots[i * SLOTS : (i + 1) * SLOTS, 0:PPAD] = hot
            hots[i * SLOTS : (i + 1) * SLOTS, PPAD:] = hot
        product = lax.dot_general(
            wscr[...], hots[...], (((1,), (1,)), ((), ())), preferred_element_type=F32
        )
        batch = step // (GB // GSTEP)
        for i in range(GSTEP):
            local = step % (GB // GSTEP) * GSTEP + i
            value = product[:, i * SLOTS : (i + 1) * SLOTS]
            top = value.astype(BF16)
            rest = (value - top.astype(F32)).astype(BF16)
            for v in range(NV):
                rows = slice(v * NU, (v + 1) * NU)
                for half in range(2):
                    start = half * WCH * SLOTS + (v // 2) * SLOTS
                    lanes = slice(half * HALF, (half + 1) * HALF)
                    alhs[batch, v % 2, local, :, start : start + HALF] = top[rows, lanes]
                    alhs[batch, v % 2, local, :, start + HALF : start + SLOTS] = rest[rows, lanes]

    for step in range(NG // GSTEP):
        alpha_rows(step)
    swaps, keeps = [], []
    for batch in range(BATCHES):
        for h in range(2):
            place = (pl.ds(batch * GB * SB, GB * SB), pl.ds(h * 128, 128))
            swaps.append(
                pltpu.make_async_remote_copy(
                    src_ref=part.at[batch, 1 - b, h],
                    dst_ref=far_ref.at[place],
                    send_sem=psem.at[batch, h],
                    recv_sem=qsem.at[batch, h],
                    device_id=partner,
                    device_id_type=MESH,
                )
            )
            keeps.append(
                pltpu.make_async_copy(part.at[batch, b, h], own_ref.at[place], ksem.at[batch, h])
            )
    small_group = lax.broadcasted_iota(jnp.int32, (GB, 128), 1) // 16
    for batch, half, q in STEPS:
        _, _, first, count = CHUNKS[q]
        if half == 0:
            own[batch].wait()
        all_blocks(q).wait_recv()
        right = []
        for w in range(first, first + count):
            right += [dst[batch, w, half * NS // 2 : (half + 1) * NS // 2].reshape(HALF, 128)] * 2
        start = half * WCH * SLOTS + first * SLOTS
        left = alhs[batch, :, :, :, start : start + count * SLOTS]
        result = jnp.dot(
            left.reshape(2 * GB * NU, count * SLOTS),
            jnp.concatenate(right, axis=0),
            preferred_element_type=F32,
        )
        if half == 1:
            result = result + fsum[batch]
        if half == 0 or first + count < WCH:
            fsum[batch] = result
            continue
        even, odd = result[0 : GB * NU], result[GB * NU :]
        xscr[...] = even + pltpu.roll(odd, 64, 1)
        for j in range(4):
            by_u = [xscr[pl.ds(8 * j + i, GB, stride=NU), :] for i in range(8)]
            total = [jnp.zeros((GB, 128), F32) for _ in range(SB)]
            for d in range(8):
                mixed = by_u[d % 8]
                for s in range(1, SB):
                    mixed = jnp.where(small_group == s, by_u[(s + d) % 8], mixed)
                moved = pltpu.roll(mixed, 16 * d, 1) if d else mixed
                for s in range(SB):
                    total[s] = jnp.where(small_group == (s + d) % 8, moved, total[s])
            for s in range(SB):
                part.at[batch, j // 2, j % 2][pl.ds(s, GB, stride=SB), :] = total[s]
        for h in range(2):
            swaps[2 * batch + h].start()
            keeps[2 * batch + h].start()

    for batch in range(BATCHES):
        in_transit(batch).wait_send()
    for q in range(len(CHUNKS)):
        all_blocks(q).wait_send()
    for swap, keep in zip(swaps, keeps):
        keep.wait()
        swap.wait()


def on_device(*operands):
    whole = pl.BlockSpec(memory_space=pl.ANY)
    own, far = pl.pallas_call(
        kernel,
        out_shape=[jax.ShapeDtypeStruct((64, 256), F32)] * 2,
        in_specs=[pl.BlockSpec(memory_space=pltpu.HBM)] * 9,
        out_specs=[pl.BlockSpec(memory_space=pltpu.VMEM)] * 2,
        scratch_shapes=[
            pltpu.VMEM((64, 256), BF16),
            pltpu.VMEM((PAIRS, PAIRS), BF16),
            pltpu.VMEM((1, BATCHES * SLOTS), jnp.int32),
            pltpu.VMEM((6, 16, EXC), jnp.int32),
            pltpu.VMEM((2, 64, 128), F32),
            pltpu.VMEM((BATCHES, WCH, NS, CAP, 128), BF16),
            pltpu.VMEM((BATCHES, WCH, NS, CAP, 128), BF16),
            pltpu.VMEM((4, 16, 256), F32),
            pltpu.VMEM((2, NV, 1, PPAD), F32),
            pltpu.VMEM((NV * NU, PPAD), BF16),
            pltpu.VMEM((PPAD, PPAD), BF16),
            pltpu.VMEM((NV * NU, 2 * PPAD), BF16),
            pltpu.VMEM((BATCHES, 2, GB, NU, WCH * 2 * SLOTS), BF16),
            pltpu.VMEM((BATCHES, WCH, len(REST), CAP, 128), BF16),
            pltpu.VMEM((GSTEP * SLOTS, 2 * PPAD), BF16),
            pltpu.VMEM((BATCHES, 2 * GB * NU, 128), F32),
            pltpu.VMEM((GB * NU, 128), F32),
            pltpu.VMEM((BATCHES, 2, 2, GB * SB, 128), F32),
            pltpu.SemaphoreType.REGULAR,
            pltpu.SemaphoreType.DMA((BATCHES,)),
            pltpu.SemaphoreType.DMA((BATCHES,)),
            pltpu.SemaphoreType.DMA((9,)),
            pltpu.SemaphoreType.DMA((len(CHUNKS),)),
            pltpu.SemaphoreType.DMA((len(CHUNKS),)),
            pltpu.SemaphoreType.DMA((BATCHES,)),
            pltpu.SemaphoreType.DMA((BATCHES, 2)),
            pltpu.SemaphoreType.DMA((BATCHES, 2)),
            pltpu.SemaphoreType.DMA((BATCHES, 2)),
        ],
        compiler_params=pltpu.CompilerParams(
            collective_id=0, has_side_effects=True, vmem_limit_bytes=28 << 20
        ),
    )(*[pltpu.with_memory_space_constraint(x, pltpu.HBM) for x in operands])
    return own + far


def solution(mesh):
    in_specs = (
        P("alpha", "beta"),
        P(),
        P("alpha", None),
        P("alpha", None),
        P("alpha", None),
        P("alpha", None),
        P("beta", None),
        P("beta", None),
        P("beta", None),
    )
    return jax.shard_map(
        on_device, mesh=mesh, in_specs=in_specs, out_specs=P("alpha", "beta"), check_vma=False
    )
```

```python
import functools

import jax
import jax.numpy as jnp
from jax import lax
from jax.experimental import pallas as pl
from jax.experimental.pallas import tpu as pltpu
from jax.sharding import PartitionSpec as P

MESH = pl.DeviceIdType.MESH
PAIRS = 484
PPAD = 512
EXC = 132
EPAD = 136
SB = 4
BATCHES = 2
CAP = 4
NV = 16
NU = 32
NG = 16
GB = 8
NS = 64
X_LINE, Y_LINE, Z_LINE = (1, 2, 3), (4, 8, 12), (16, 32, 48)
LINES = X_LINE + Y_LINE + Z_LINE


def dims_of(k):
    return (k % 4 > 0) + (k // 4 % 4 > 0) + (k // 16 > 0)


PLANES = tuple(k for k in range(1, 64) if dims_of(k) == 2)
REST = tuple(k for k in range(1, 64) if dims_of(k) == 3)
NEAR = LINES + PLANES


def first_leg(k):
    digits = (k % 4, k // 4 % 4 * 4, k // 16 * 16)
    return digits[sum((k % 4, k // 4 % 4, k // 16)) % 3]


ORDER = (0,) + LINES + PLANES[:22] + REST + PLANES[22:]
POS = tuple(ORDER.index(k) for k in range(64))
CHUNKS = (
    (NEAR, 0, 0, 8),
    (NEAR, 1, 0, 8),
    (REST, 0, 0, 8),
    (REST, 1, 0, 4),
    (REST, 1, 4, 4),
)
STEPS = ((0, 0, 0), (0, 1, 2), (1, 0, 1), (1, 1, 3), (1, 1, 4))
WCH = 8
SLOTS = NS * CAP
GSTEP = 4
HALF = SLOTS // 2
F32 = jnp.float32
BF16 = jnp.bfloat16


def kernel(
    coeffs_ref,
    integrals_ref,
    send_ref,
    aslot_ref,
    apair_ref,
    apar_ref,
    bpair_ref,
    btarget_ref,
    bpar_ref,
    own_ref,
    far_ref,
    coeffs,
    integrals,
    sends,
    small,
    cscr,
    src,
    dst,
    tab,
    codes,
    tscr,
    ipad,
    wscr,
    alhs,
    transit,
    hots,
    fsum,
    xscr,
    part,
    near_sem,
    tsend,
    trecv,
    insem,
    ssem,
    rsem,
    lsem,
    ksem,
    psem,
    qsem,
):
    a = lax.axis_index("alpha")
    b = lax.axis_index("beta")
    partner = (a, 1 - b)

    here = (lax.div(a, 16), lax.rem(lax.div(a, 4), 4), lax.rem(a, 4))
    steps = [[lax.rem(place + i, 4) * scale for i in range(4)] for place, scale in zip(here, (16, 4, 1))]

    def peer(k):
        return steps[0][k // 16] + (steps[1][k // 4 % 4] + steps[2][k % 4])

    barrier = pltpu.get_barrier_semaphore()
    loads = [
        pltpu.make_async_copy(ref, to, insem.at[i])
        for i, (ref, to) in enumerate(
            [(coeffs_ref, coeffs), (send_ref, sends)]
            + [
                (ref, small.at[i])
                for i, ref in enumerate(
                    [bpair_ref, btarget_ref, bpar_ref, apair_ref, aslot_ref, apar_ref]
                )
            ]
            + [(integrals_ref, integrals)]
        )
    ]
    for load in loads:
        load.start()

    def tell(semaphore, k):
        pl.semaphore_signal(semaphore, inc=1, device_id=(peer(k), b), device_id_type=MESH)

    for k in LINES:
        tell(barrier, k)
    pl.semaphore_signal(barrier, inc=1, device_id=partner, device_id_type=MESH)

    loads[0].wait()
    loads[1].wait()
    for h in range(2):
        cscr[h] = coeffs[:, h * 128 : (h + 1) * 128].astype(F32)
    lane_group = lax.broadcasted_iota(jnp.int32, (16, 128), 1) // 16
    pieces = [
        [cscr.at[h][pl.ds(s, 16, stride=SB), :] for h in range(2)] for s in range(SB)
    ]
    columns = []
    for w in range(WCH):
        value = jnp.zeros((16, 128), F32)
        for par in range(2):
            v = 2 * w + par
            for s in range(SB):
                shift = ((par * 4 + s) - (v % 8)) % 8 * 16
                piece = pieces[s][v // 8]
                moved = pltpu.roll(piece, shift, 1) if shift else piece
                value = jnp.where(lane_group == par * 4 + s, moved, value)
        columns.append(value.astype(BF16))
    blocks = jnp.concatenate(columns, axis=1)
    for batch in range(BATCHES):
        wanted = sends[:, pl.ds(batch * SLOTS, SLOTS)]
        hot = (lax.broadcasted_iota(jnp.int32, (16, SLOTS), 0) == wanted).astype(F32)
        picked = jnp.dot(hot.T.astype(BF16), blocks, preferred_element_type=F32).astype(BF16)
        for w in range(WCH):
            src[batch, w] = picked[:, w * 128 : (w + 1) * 128].reshape(NS, CAP, 128)

    pl.semaphore_wait(barrier, len(LINES) + 1)

    def first_copy(batch, i):
        to, relay = peer(REST[i]), peer(first_leg(REST[i]))
        return pltpu.make_async_remote_copy(
            src_ref=src.at[batch, :, to],
            dst_ref=transit.at[batch, :, i],
            send_sem=tsend.at[batch],
            recv_sem=trecv.at[batch],
            device_id=(relay, b),
            device_id_type=MESH,
        )

    def in_transit(batch):
        return pltpu.make_async_remote_copy(
            src_ref=src.at[batch, :, pl.ds(0, len(REST))],
            dst_ref=transit.at[batch],
            send_sem=tsend.at[batch],
            recv_sem=trecv.at[batch],
            device_id=partner,
            device_id_type=MESH,
        )

    def forward(q, i):
        _, batch, first, count = CHUNKS[q]
        cols, k = pl.ds(first, count), REST[i]
        return pltpu.make_async_remote_copy(
            src_ref=transit.at[batch, cols, i],
            dst_ref=dst.at[batch, cols, POS[k]],
            send_sem=ssem.at[q],
            recv_sem=rsem.at[q],
            device_id=(peer(k - first_leg(k)), b),
            device_id_type=MESH,
        )

    def block_copy(q, k):
        _, batch, first, count = CHUNKS[q]
        cols, to = pl.ds(first, count), peer(k)
        return pltpu.make_async_remote_copy(
            src_ref=src.at[batch, cols, to],
            dst_ref=dst.at[batch, cols, POS[k]],
            send_sem=ssem.at[q],
            recv_sem=rsem.at[q],
            device_id=(to, b),
            device_id_type=MESH,
        )

    def all_blocks(q):
        peers, batch, first, count = CHUNKS[q]
        cols = pl.ds(first, count)
        return pltpu.make_async_remote_copy(
            src_ref=src.at[batch, cols, pl.ds(0, len(peers))],
            dst_ref=dst.at[batch, cols, pl.ds(0, len(peers))],
            send_sem=ssem.at[q],
            recv_sem=rsem.at[q],
            device_id=partner,
            device_id_type=MESH,
        )

    def send(q, k):
        block_copy(q, k).start()

    def send_all(peers):
        for q, chunk in enumerate(CHUNKS):
            for k in peers:
                if k in chunk[0]:
                    send(q, k)

    for k in Y_LINE + Z_LINE:
        tell(near_sem, k)
    for batch in range(BATCHES):
        for i in range(len(REST)):
            first_copy(batch, i).start()
    send_all(LINES)
    own = [
        pltpu.make_async_copy(src.at[batch, :, a], dst.at[batch, :, POS[0]], lsem.at[batch])
        for batch in range(BATCHES)
    ]
    for copy in own:
        copy.start()

    tab[...] = jnp.full(tab.shape, -1.0, F32)
    for load in loads[2:]:
        load.wait()
    for side in range(2):
        pair, place, parity = (small[3 * side + i] for i in range(3))
        if side == 1:
            sender = lax.shift_right_logical(place, 2)
            apart = (
                ((here[0] - lax.shift_right_logical(sender, 4)) & 3) * 16
                + ((here[1] - (lax.shift_right_logical(sender, 2) & 3)) & 3) * 4
                + ((here[2] - (sender & 3)) & 3)
            )
            slot = place & 3
            for k in range(NS):
                slot = slot + jnp.where(apart == k, POS[k] * CAP, 0)
            place = slot
        tab[2 * side, :, 0:EXC] = pair.astype(F32)
        tab[2 * side + 1, :, 0:EXC] = ((1 - 2 * parity) * (place + 1)).astype(F32)
    pair_lane = lax.broadcasted_iota(jnp.int32, (EPAD, PPAD), 1).astype(F32)
    for side in range(2):
        pair_cols = tab[2 * side].T[0:EPAD]
        code_cols = tab[2 * side + 1].T[0:EPAD]
        for row in range(NV):
            hit = pair_cols[:, row : row + 1] == pair_lane
            codes[side, row] = jnp.sum(
                jnp.where(hit, code_cols[:, row : row + 1], 0.0), axis=0, keepdims=True
            )

    def signed_hot(code, count):
        place = (lax.broadcasted_iota(jnp.int32, (count, PPAD), 0) + 1).astype(F32)
        return (jnp.where(code == place, 1.0, 0.0) - jnp.where(code == -place, 1.0, 0.0)).astype(
            BF16
        )

    def beta_row(v, carry):
        tscr[pl.ds(pl.multiple_of(v * NU, NU), NU), :] = signed_hot(codes[0, v], NU)
        return carry

    lax.fori_loop(0, NV, beta_row, 0)
    ipad[...] = jnp.zeros(ipad.shape, BF16)
    ipad[0:PAIRS, 0:PAIRS] = integrals[...]
    table = jnp.dot(tscr[...], ipad[...], preferred_element_type=F32)
    high = table.astype(BF16)
    wscr[:, 0:PPAD] = high
    wscr[:, PPAD:] = (table - high.astype(F32)).astype(BF16)

    def alpha_rows(step):
        for i in range(GSTEP):
            hot = signed_hot(codes[1, step * GSTEP + i], SLOTS)
            hots[i * SLOTS : (i + 1) * SLOTS, 0:PPAD] = hot
            hots[i * SLOTS : (i + 1) * SLOTS, PPAD:] = hot
        product = lax.dot_general(
            wscr[...], hots[...], (((1,), (1,)), ((), ())), preferred_element_type=F32
        )
        batch = step // (GB // GSTEP)
        for i in range(GSTEP):
            local = step % (GB // GSTEP) * GSTEP + i
            value = product[:, i * SLOTS : (i + 1) * SLOTS]
            top = value.astype(BF16)
            rest = (value - top.astype(F32)).astype(BF16)
            for v in range(NV):
                rows = slice(v * NU, (v + 1) * NU)
                for half in range(2):
                    start = half * WCH * SLOTS + (v // 2) * SLOTS
                    lanes = slice(half * HALF, (half + 1) * HALF)
                    alhs[batch, v % 2, local, :, start : start + HALF] = top[rows, lanes]
                    alhs[batch, v % 2, local, :, start + HALF : start + SLOTS] = rest[rows, lanes]

    pl.semaphore_wait(near_sem, len(Y_LINE + Z_LINE))
    for batch in range(BATCHES):
        for k in PLANES:
            send(batch, k)
        if batch == 0:
            alpha_rows(0)
        in_transit(batch).wait_recv()
        for q, chunk in enumerate(CHUNKS):
            if chunk[0] == REST and chunk[1] == batch:
                for i in range(len(REST)):
                    forward(q, i).start()

    for step in range(1, NG // GSTEP):
        alpha_rows(step)
    swaps, keeps = [], []
    for batch in range(BATCHES):
        for h in range(2):
            place = (pl.ds(batch * GB * SB, GB * SB), pl.ds(h * 128, 128))
            swaps.append(
                pltpu.make_async_remote_copy(
                    src_ref=part.at[batch, 1 - b, h],
                    dst_ref=far_ref.at[place],
                    send_sem=psem.at[batch, h],
                    recv_sem=qsem.at[batch, h],
                    device_id=partner,
                    device_id_type=MESH,
                )
            )
            keeps.append(
                pltpu.make_async_copy(part.at[batch, b, h], own_ref.at[place], ksem.at[batch, h])
            )
    small_group = lax.broadcasted_iota(jnp.int32, (GB, 128), 1) // 16
    for batch, half, q in STEPS:
        _, _, first, count = CHUNKS[q]
        if half == 0:
            own[batch].wait()
        all_blocks(q).wait_recv()
        right = []
        for w in range(first, first + count):
            right += [dst[batch, w, half * NS // 2 : (half + 1) * NS // 2].reshape(HALF, 128)] * 2
        start = half * WCH * SLOTS + first * SLOTS
        left = alhs[batch, :, :, :, start : start + count * SLOTS]
        result = jnp.dot(
            left.reshape(2 * GB * NU, count * SLOTS),
            jnp.concatenate(right, axis=0),
            preferred_element_type=F32,
        )
        if half == 1:
            result = result + fsum[batch]
        if half == 0 or first + count < WCH:
            fsum[batch] = result
            continue
        even, odd = result[0 : GB * NU], result[GB * NU :]
        xscr[...] = even + pltpu.roll(odd, 64, 1)
        for j in range(4):
            by_u = [xscr[pl.ds(8 * j + i, GB, stride=NU), :] for i in range(8)]
            total = [jnp.zeros((GB, 128), F32) for _ in range(SB)]
            for d in range(8):
                mixed = by_u[d % 8]
                for s in range(1, SB):
                    mixed = jnp.where(small_group == s, by_u[(s + d) % 8], mixed)
                moved = pltpu.roll(mixed, 16 * d, 1) if d else mixed
                for s in range(SB):
                    total[s] = jnp.where(small_group == (s + d) % 8, moved, total[s])
            for s in range(SB):
                part.at[batch, j // 2, j % 2][pl.ds(s, GB, stride=SB), :] = total[s]
        for h in range(2):
            swaps[2 * batch + h].start()
            keeps[2 * batch + h].start()

    for batch in range(BATCHES):
        in_transit(batch).wait_send()
    for q in range(len(CHUNKS)):
        all_blocks(q).wait_send()
    for swap, keep in zip(swaps, keeps):
        keep.wait()
        swap.wait()


def on_device(*operands):
    whole = pl.BlockSpec(memory_space=pl.ANY)
    own, far = pl.pallas_call(
        kernel,
        out_shape=[jax.ShapeDtypeStruct((64, 256), F32)] * 2,
        in_specs=[pl.BlockSpec(memory_space=pltpu.HBM)] * 9,
        out_specs=[pl.BlockSpec(memory_space=pltpu.VMEM)] * 2,
        scratch_shapes=[
            pltpu.VMEM((64, 256), BF16),
            pltpu.VMEM((PAIRS, PAIRS), BF16),
            pltpu.VMEM((1, BATCHES * SLOTS), jnp.int32),
            pltpu.VMEM((6, 16, EXC), jnp.int32),
            pltpu.VMEM((2, 64, 128), F32),
            pltpu.VMEM((BATCHES, WCH, NS, CAP, 128), BF16),
            pltpu.VMEM((BATCHES, WCH, NS, CAP, 128), BF16),
            pltpu.VMEM((4, 16, 256), F32),
            pltpu.VMEM((2, NV, 1, PPAD), F32),
            pltpu.VMEM((NV * NU, PPAD), BF16),
            pltpu.VMEM((PPAD, PPAD), BF16),
            pltpu.VMEM((NV * NU, 2 * PPAD), BF16),
            pltpu.VMEM((BATCHES, 2, GB, NU, WCH * 2 * SLOTS), BF16),
            pltpu.VMEM((BATCHES, WCH, len(REST), CAP, 128), BF16),
            pltpu.VMEM((GSTEP * SLOTS, 2 * PPAD), BF16),
            pltpu.VMEM((BATCHES, 2 * GB * NU, 128), F32),
            pltpu.VMEM((GB * NU, 128), F32),
            pltpu.VMEM((BATCHES, 2, 2, GB * SB, 128), F32),
            pltpu.SemaphoreType.REGULAR,
            pltpu.SemaphoreType.DMA((BATCHES,)),
            pltpu.SemaphoreType.DMA((BATCHES,)),
            pltpu.SemaphoreType.DMA((9,)),
            pltpu.SemaphoreType.DMA((len(CHUNKS),)),
            pltpu.SemaphoreType.DMA((len(CHUNKS),)),
            pltpu.SemaphoreType.DMA((BATCHES,)),
            pltpu.SemaphoreType.DMA((BATCHES, 2)),
            pltpu.SemaphoreType.DMA((BATCHES, 2)),
            pltpu.SemaphoreType.DMA((BATCHES, 2)),
        ],
        compiler_params=pltpu.CompilerParams(
            collective_id=0, has_side_effects=True, vmem_limit_bytes=28 << 20
        ),
    )(*[pltpu.with_memory_space_constraint(x, pltpu.HBM) for x in operands])
    return own + far


def solution(mesh):
    in_specs = (
        P("alpha", "beta"),
        P(),
        P("alpha", None),
        P("alpha", None),
        P("alpha", None),
        P("alpha", None),
        P("beta", None),
        P("beta", None),
        P("beta", None),
    )
    return jax.shard_map(
        on_device, mesh=mesh, in_specs=in_specs, out_specs=P("alpha", "beta"), check_vma=False
    )
```
